32 devices in a mesh: dp: 16 (over z, x, core), mp: 2 (over y).
Axes of the slice: x: 2, y: 2, z: 4, core: 2. Of those that a mesh axis runs over, the one named last changes fastest.
Arguments:
- layer_in: bfloat16 [4096, 2048], P('dp'), may hold values from -6 to 6
- out_grad: bfloat16 [4096, 2048], P('dp'), may hold values from -6 to 6
- norm_gain: bfloat16 [2, 2048], P(None, 'dp'), may hold values from 0.5 to 1.5
- norm_bias: bfloat16 [2, 2048], P(None, 'dp'), may hold values from -1.5 to 1.5
- qkv_weight: bfloat16 [3, 2048, 2048], P(None, 'dp', 'mp'), may hold values from -0.125 to 0.125
- qkv_bias: bfloat16 [3, 8, 256], P(None, 'mp', 'dp'), may hold values from -12 to 12
- out_weight: bfloat16 [2048, 2048], P('mp', 'dp'), may hold values from -1 to 1
- attn_bias: bfloat16 [2048], P('dp'), may hold values from -1.5 to 1.5
- up_weight: bfloat16 [2048, 8192], P('dp', 'mp'), may hold values from -0.125 to 0.125
- up_bias: bfloat16 [64, 128], P('mp', 'dp'), may hold values from -1.5 to 1.5
- down_weight: bfloat16 [8192, 2048], P('mp', 'dp'), may hold values from -0.0625 to 0.0625
- mlp_bias: bfloat16 [2048], P('dp'), may hold values from -1.5 to 1.5
Outputs:
- layer_out: float32 [4096, 2048], P('dp')
- in_grad: float32 [4096, 2048], P('dp')
- gain_grad: float32 [2, 2048], P(None, 'dp')
- shift_grad: float32 [2, 2048], P(None, 'dp')
- qkv_grad: float32 [3, 2048, 2048], P(None, 'dp', 'mp')
- qkv_bias_grad: float32 [3, 8, 256], P(None, 'mp', 'dp')
- out_weight_grad: float32 [2048, 2048], P('mp', 'dp')
- out_bias_grad: float32 [2048], P('dp')
- up_grad: float32 [2048, 8192], P('dp', 'mp')
- up_bias_grad: float32 [64, 128], P('mp', 'dp')
- down_grad: float32 [8192, 2048], P('mp', 'dp')
The draws below stay inside these ranges and needn't reach their ends.
All inputs are finite; a program needn't handle non-finite values.
Results may differ from the reference program's by a relative error of at most 0.0095.
The reference program's roundings to bfloat16 on the way count: a program that leaves them out, or rounds other values in their place, can miss the bound.
Values may be sent and summed in bfloat16 or wider, within the bound.
No kernel may reach another device: no remote copies, remote signals or barrier semaphores. Data moves between devices by JAX's collectives and lax.ppermute only.
A program may use at most 256 MiB of HBM per device.

```python
import math
import jax
import jax.numpy as jnp
from jax import lax

D = 2048
HEADS = 8
HEAD = 256
ROT = 64
FF = 8192
SEQ = 256
SEQ_DEV = 1
TOKENS = 4096


def draw_qkv_bias(key, part):
    noise_key = jax.random.fold_in(key, 0)
    baseline = jnp.clip(0.3 * jax.random.normal(noise_key, (3, HEADS, HEAD), jnp.float32), -1.5, 1.5)
    return baseline.astype(jnp.bfloat16)


def block_levels(key, shape, pieces, smallest, largest):
    def one(axis_at, shards_of):
        draws = jax.random.uniform(jax.random.fold_in(jax.random.fold_in(key, 6), axis_at), (shards_of,), jnp.float32, smallest / len(pieces), largest / len(pieces))
        return jnp.repeat(jnp.exp(draws), shape[axis_at] // shards_of).reshape((-1,) + (1,) * (len(shape) - axis_at - 1))

    level = one(*pieces[0])
    for cut in pieces[1:]:
        level = level * one(*cut)
    return level


def normal_values(key, extent, spread, limit, cuts=(), kind=jnp.bfloat16):
    values = jax.random.normal(key, extent, jnp.float32) * spread
    if len(cuts) > 0:
        values = block_levels(key, extent, cuts, -0.22, 0.18) * values
    return jnp.clip(values, min=-limit, max=limit).astype(kind)


def setup_inputs(seed: int = 0) -> dict:
    keys = jax.random.split(jax.random.key(seed), 13)
    return {
        "layer_in": normal_values(keys[0], (TOKENS, D), 1.0, 6.0, ((0, 16),)),
        "out_grad": normal_values(keys[1], (TOKENS, D), 1.0, 6.0, ((0, 16),)),
        "norm_gain": jnp.clip(1.0 + 0.1 * jax.random.normal(keys[2], (2, D), jnp.float32), 0.5, 1.5).astype(jnp.bfloat16),
        "norm_bias": normal_values(keys[3], (2, D), 0.3, 1.5, ((1, 16),)),
        "qkv_weight": normal_values(keys[4], (3, D, D), D ** -0.5, 0.125, ((1, 16), (2, 2))),
        "qkv_bias": draw_qkv_bias(jax.random.fold_in(keys[12], 71), 0),
        "out_weight": normal_values(keys[6], (D, D), (D // 64) ** -0.5, 1.0, ((0, 2), (1, 16))),
        "attn_bias": normal_values(keys[7], (D,), 0.3, 1.5, ((0, 16),)),
        "up_weight": normal_values(keys[8], (D, FF), D ** -0.5, 0.125, ((0, 16), (1, 2))),
        "up_bias": normal_values(keys[9], (FF // 128, 128), 0.3, 1.5, ((0, 2), (1, 16))),
        "down_weight": normal_values(keys[10], (FF, D), FF ** -0.5, 0.0625, ((0, 2), (1, 16))),
        "mlp_bias": normal_values(keys[11], (D,), 0.3, 1.5, ((0, 16),)),
    }


EPS = 1e-05
NORMAL_PEAK = 0.3989422804014327
ROOT_HALF = 0.7071067811865476

def normalize(rows_in):
    mean_row = lax.optimization_barrier(jnp.mean(rows_in, axis=-1, keepdims=True))
    centred = rows_in - mean_row
    variance = lax.optimization_barrier(jnp.mean(centred * centred, axis=-1, keepdims=True))
    inv_std = lax.rsqrt(variance + EPS)
    return (centred * inv_std, inv_std)

def rotary(length, half_rot, full_rot):
    position = jnp.arange(length, dtype=jnp.float32)[:, None]
    exponent = jnp.arange(half_rot, dtype=jnp.float32) * (2.0 / full_rot)
    angle = position * jnp.exp(-math.log(10000.0) * exponent)[None, :]
    return (jnp.cos(angle), jnp.sin(angle))

def turn(tensor, cosine, sine, sign):
    half_rot = cosine.shape[-1]
    lead_part = tensor[..., :half_rot]
    next_part = tensor[..., half_rot:2 * half_rot]
    rest_part = tensor[..., 2 * half_rot:]
    cos_rows = cosine[None, :, None, :]
    sin_rows = sign * sine[None, :, None, :]
    return jnp.concatenate([lead_part * cos_rows - next_part * sin_rows, next_part * cos_rows + lead_part * sin_rows, rest_part], axis=-1)

def causal_scores(queries, keys_rot):
    scale = HEAD ** (-0.5)
    scores = jnp.einsum('bqhe,bkhe->bhqk', queries.astype(jnp.float32), keys_rot.astype(jnp.float32)) * scale
    length = scores.shape[-1]
    causal = lax.broadcasted_iota(jnp.int32, (length, length), 0) >= lax.broadcasted_iota(jnp.int32, (length, length), 1)
    return jnp.where(causal, scores, -jnp.inf)

def attend(queries, keys_rot, values):
    scores = causal_scores(queries, keys_rot)
    top_score = lax.optimization_barrier(jnp.max(scores, axis=-1, keepdims=True))
    total = lax.optimization_barrier(jnp.sum(jnp.exp(scores - top_score), axis=-1, keepdims=True))
    log_total = top_score + jnp.log(total)
    probs = jnp.exp(scores - log_total).astype(jnp.bfloat16)
    context = jnp.einsum('bhqk,bkhe->bqhe', probs.astype(jnp.float32), values.astype(jnp.float32))
    return (context.astype(jnp.bfloat16), log_total)

def attend_back(queries, keys_rot, values, log_total, grad_context):
    scale = HEAD ** (-0.5)
    prob_full = jnp.exp(causal_scores(queries, keys_rot) - log_total)
    probs = prob_full.astype(jnp.bfloat16).astype(jnp.float32)
    context_f = grad_context.astype(jnp.float32)
    grad_values = jnp.einsum('bhqk,bqhe->bkhe', probs, context_f)
    grad_probs = jnp.einsum('bqhe,bkhe->bhqk', context_f, values.astype(jnp.float32))
    grad_scores = prob_full * (grad_probs - lax.optimization_barrier(jnp.sum(prob_full * grad_probs, axis=-1, keepdims=True)))
    scores_half = grad_scores.astype(jnp.bfloat16).astype(jnp.float32)
    grad_queries = jnp.einsum('bhqk,bkhe->bqhe', scores_half, keys_rot.astype(jnp.float32)) * scale
    grad_keys = jnp.einsum('bhqk,bqhe->bkhe', scores_half, queries.astype(jnp.float32)) * scale
    return (grad_queries, grad_keys, grad_values)

def gelu_slope(value):
    return 0.5 * (1.0 + lax.erf(value * ROOT_HALF)) + value * jnp.exp(-0.5 * value * value) * NORMAL_PEAK

def one_block(block_in, block_grad, norm_gain, norm_bias, qkv_weight, qkv_bias, out_weight, attn_bias, up_weight, up_bias, down_weight, mlp_bias):
    row_count = block_in.shape[0]
    seq_count = row_count // SEQ
    inputs = block_in.astype(jnp.float32)
    unit_rows, inv_std = normalize(inputs)
    gains = norm_gain.astype(jnp.float32)
    shifts = norm_bias.astype(jnp.float32)
    normed_attn = (unit_rows * gains[0] + shifts[0]).astype(jnp.bfloat16)
    normed_mlp = (unit_rows * gains[1] + shifts[1]).astype(jnp.bfloat16)
    cosine, sine = rotary(SEQ, ROT // 2, ROT)
    projected = [jnp.dot(normed_attn, qkv_weight[index], preferred_element_type=jnp.float32) + qkv_bias[index].reshape(D).astype(jnp.float32) for index in range(3)]
    shaped = [item.reshape(seq_count, SEQ, HEADS, HEAD) for item in projected]
    queries = turn(shaped[0], cosine, sine, 1.0).astype(jnp.bfloat16)
    keys_rot = turn(shaped[1], cosine, sine, 1.0).astype(jnp.bfloat16)
    values = shaped[2].astype(jnp.bfloat16)
    context, log_total = attend(queries, keys_rot, values)
    context_rows = context.reshape(row_count, D)
    pre_act = jnp.dot(normed_mlp, up_weight, preferred_element_type=jnp.float32) + up_bias.reshape(FF).astype(jnp.float32)
    activated = jax.nn.gelu(pre_act, approximate=False).astype(jnp.bfloat16)
    branch_sum = jnp.dot(context_rows, out_weight, preferred_element_type=jnp.float32) + jnp.dot(activated, down_weight, preferred_element_type=jnp.float32)
    layer_out = inputs + branch_sum + attn_bias.astype(jnp.float32) + mlp_bias.astype(jnp.float32)
    out_bias_grad = lax.optimization_barrier(jnp.sum(block_grad.astype(jnp.float32), axis=0))
    down_grad = jnp.dot(activated.T, block_grad, preferred_element_type=jnp.float32)
    grad_act = jnp.dot(block_grad, down_weight.T, preferred_element_type=jnp.float32)
    grad_pre = grad_act * gelu_slope(pre_act)
    up_bias_grad = lax.optimization_barrier(jnp.sum(grad_pre, axis=0)).reshape(up_bias.shape)
    pre_half = grad_pre.astype(jnp.bfloat16)
    up_grad = jnp.dot(normed_mlp.T, pre_half, preferred_element_type=jnp.float32)
    grad_normed_mlp = jnp.dot(pre_half, up_weight.T, preferred_element_type=jnp.float32)
    out_weight_grad = jnp.dot(context_rows.T, block_grad, preferred_element_type=jnp.float32)
    grad_context = jnp.dot(block_grad, out_weight.T, preferred_element_type=jnp.float32).astype(jnp.bfloat16)
    grad_context = grad_context.reshape(seq_count, SEQ, HEADS, HEAD)
    grad_queries, grad_keys, grad_values = attend_back(queries, keys_rot, values, log_total, grad_context)
    grad_proj = [turn(grad_queries, cosine, sine, -1.0).reshape(row_count, D), turn(grad_keys, cosine, sine, -1.0).reshape(row_count, D), grad_values.reshape(row_count, D)]
    qkv_bias_grad = jnp.stack([lax.optimization_barrier(jnp.sum(item, axis=0)) for item in grad_proj]).reshape(3, HEADS, HEAD)
    proj_half = [item.astype(jnp.bfloat16) for item in grad_proj]
    qkv_grad = jnp.stack([jnp.dot(normed_attn.T, item, preferred_element_type=jnp.float32) for item in proj_half])
    grad_normed_attn = jnp.dot(proj_half[0], qkv_weight[0].T, preferred_element_type=jnp.float32)
    grad_normed_attn = grad_normed_attn + jnp.dot(proj_half[1], qkv_weight[1].T, preferred_element_type=jnp.float32)
    grad_normed_attn = grad_normed_attn + jnp.dot(proj_half[2], qkv_weight[2].T, preferred_element_type=jnp.float32)
    gain_grad = jnp.stack([lax.optimization_barrier(jnp.sum(grad_normed_attn * unit_rows, axis=0)), lax.optimization_barrier(jnp.sum(grad_normed_mlp * unit_rows, axis=0))])
    shift_grad = jnp.stack([lax.optimization_barrier(jnp.sum(grad_normed_attn, axis=0)), lax.optimization_barrier(jnp.sum(grad_normed_mlp, axis=0))])
    grad_unit = grad_normed_attn * gains[0] + grad_normed_mlp * gains[1]
    in_grad = block_grad.astype(jnp.float32) + inv_std * (grad_unit - lax.optimization_barrier(jnp.mean(grad_unit, axis=-1, keepdims=True)) - unit_rows * lax.optimization_barrier(jnp.mean(grad_unit * unit_rows, axis=-1, keepdims=True)))
    grads = (gain_grad, shift_grad, qkv_grad, qkv_bias_grad, out_weight_grad, out_bias_grad, up_grad, up_bias_grad, down_grad)
    return (layer_out, in_grad, grads)

def add_pair(left, right):
    return left + right

def reference(layer_in, out_grad, norm_gain, norm_bias, qkv_weight, qkv_bias, out_weight, attn_bias, up_weight, up_bias, down_weight, mlp_bias):
    row_count = SEQ * SEQ_DEV
    blocks = layer_in.shape[0] // row_count
    zeros = (jnp.zeros((2, D), jnp.float32), jnp.zeros((2, D), jnp.float32), jnp.zeros((3, D, D), jnp.float32), jnp.zeros((3, HEADS, HEAD), jnp.float32), jnp.zeros((D, D), jnp.float32), jnp.zeros((D,), jnp.float32), jnp.zeros((D, FF), jnp.float32), jnp.zeros((FF // 128, 128), jnp.float32), jnp.zeros((FF, D), jnp.float32))

    def step(carry, block):
        block_in, block_grad = block
        layer_out, in_grad, grads = one_block(block_in, block_grad, norm_gain, norm_bias, qkv_weight, qkv_bias, out_weight, attn_bias, up_weight, up_bias, down_weight, mlp_bias)
        return (jax.tree.map(add_pair, carry, grads), (layer_out, in_grad))
    totals, results = lax.scan(step, zeros, (layer_in.reshape(blocks, row_count, D), out_grad.reshape(blocks, row_count, D)))
    layer_out = results[0].reshape(blocks * row_count, D)
    in_grad = results[1].reshape(blocks * row_count, D)
    return (layer_out, in_grad, totals[0], totals[1], totals[2], totals[3], totals[4], totals[5], totals[6], totals[7], totals[8])
```

```python
import math

import jax
import jax.numpy as jnp
from jax import lax
from jax.sharding import Mesh
from jax.sharding import PartitionSpec as P

HEAD = 256
ROT = 64
SEQ = 256

EPS = 1e-05
NORMAL_PEAK = 0.3989422804014327
ROOT_HALF = 0.7071067811865476


BF = jnp.bfloat16
F32 = jnp.float32


def matmul(left, right, left_dim, right_dim):
    return lax.dot_general(
        left, right, (((left_dim,), (right_dim,)), ((), ())), preferred_element_type=F32
    )


def normalize(rows_in):
    mean_row = jnp.mean(rows_in, axis=-1, keepdims=True)
    centred = rows_in - mean_row
    variance = jnp.mean(centred * centred, axis=-1, keepdims=True)
    inv_std = lax.rsqrt(variance + EPS)
    return (centred * inv_std, inv_std)


def rotary(position, half_rot, full_rot):
    exponent = jnp.arange(half_rot, dtype=F32) * (2.0 / full_rot)
    angle = position.astype(F32)[:, None] * jnp.exp(-math.log(10000.0) * exponent)[None, :]
    return (jnp.cos(angle), jnp.sin(angle))


def turn(tensor, cosine, sine, sign):
    half_rot = cosine.shape[-1]
    lead_part = tensor[..., :half_rot]
    next_part = tensor[..., half_rot : 2 * half_rot]
    rest_part = tensor[..., 2 * half_rot :]
    cos_rows = cosine[None, :, None, :]
    sin_rows = sign * sine[None, :, None, :]
    return jnp.concatenate(
        [
            lead_part * cos_rows - next_part * sin_rows,
            next_part * cos_rows + lead_part * sin_rows,
            rest_part,
        ],
        axis=-1,
    )


def causal_scores(queries, keys_rot, position):
    scale = HEAD ** (-0.5)
    scores = (
        jnp.einsum("bqhe,bkhe->bhqk", queries, keys_rot, preferred_element_type=F32) * scale
    )
    causal = position[:, None] >= position[None, :]
    return jnp.where(causal, scores, -jnp.inf)


def attend(queries, keys_rot, values, position):
    scores = causal_scores(queries, keys_rot, position)
    top_score = jnp.max(scores, axis=-1, keepdims=True)
    total = jnp.sum(jnp.exp(scores - top_score), axis=-1, keepdims=True)
    log_total = top_score + jnp.log(total)
    probs = jnp.exp(scores - log_total).astype(BF)
    context = jnp.einsum("bhqk,bkhe->bqhe", probs, values, preferred_element_type=F32)
    return (context.astype(BF), log_total)


def attend_back(queries, keys_rot, values, log_total, grad_context, position):
    scale = HEAD ** (-0.5)
    prob_full = jnp.exp(causal_scores(queries, keys_rot, position) - log_total)
    probs = prob_full.astype(BF)
    grad_values = jnp.einsum("bhqk,bqhe->bkhe", probs, grad_context, preferred_element_type=F32)
    grad_probs = jnp.einsum("bqhe,bkhe->bhqk", grad_context, values, preferred_element_type=F32)
    grad_scores = prob_full * (grad_probs - jnp.sum(prob_full * grad_probs, axis=-1, keepdims=True))
    scores_half = grad_scores.astype(BF)
    grad_queries = (
        jnp.einsum("bhqk,bkhe->bqhe", scores_half, keys_rot, preferred_element_type=F32) * scale
    )
    grad_keys = (
        jnp.einsum("bhqk,bqhe->bkhe", scores_half, queries, preferred_element_type=F32) * scale
    )
    return (grad_queries, grad_keys, grad_values)


def gelu_slope(value):
    return (
        0.5 * (1.0 + lax.erf(value * ROOT_HALF))
        + value * jnp.exp(-0.5 * value * value) * NORMAL_PEAK
    )


def make_body(parts, lanes):
    def shift(array, step):
        return lax.ppermute(array, "k", [(i, (i + step) % parts) for i in range(parts)])

    def hop(array, pairs):
        return lax.ppermute(array, "k", [(a, b) for a, b in pairs])

    up_pairs = [(i, i + 1) for i in range(parts - 1)]
    down_pairs = [(i + 1, i) for i in range(parts - 1)]
    far_pairs = [(i, (i + 2) % parts) for i in range(parts)]

    def swap(array):
        return lax.ppermute(array, "mp", [(0, 1), (1, 0)])

    def send_pieces(pieces):
        rank = lax.axis_index("k")
        arrived = [lax.dynamic_index_in_dim(pieces, rank, 0, keepdims=True)]
        for step in range(1, parts):
            sent = lax.dynamic_index_in_dim(pieces, (rank + step) % parts, 0, keepdims=True)
            arrived.append(shift(sent, step))
        return arrived

    def place(arrived):
        rank = lax.axis_index("k")
        result = jnp.zeros((parts, *arrived[0].shape[1:]), arrived[0].dtype)
        for step, block in enumerate(arrived):
            result = lax.dynamic_update_slice_in_dim(
                result, block, (rank + parts - step) % parts, 0
            )
        return result

    def body(
        layer_in,
        out_grad,
        norm_gain,
        norm_bias,
        qkv_weight,
        qkv_bias,
        out_weight,
        attn_bias,
        up_weight,
        up_bias,
        down_weight,
        mlp_bias,
    ):
        side = lax.axis_index("mp")
        row_count, width = layer_in.shape
        slab = norm_gain.shape[1]
        seq_own = row_count // SEQ
        half = SEQ // 2
        heads = qkv_bias.shape[1]
        head_own = heads // parts
        attn_units = head_own * HEAD
        hidden = up_weight.shape[1] // parts
        up_rows = up_bias.shape[0] // parts
        tokens = parts * row_count
        devices = parts * lanes
        piece_width = 4 * attn_units
        tail = qkv_bias.shape[2]
        up_tail = up_bias.shape[1]
        bias_size = 3 * head_own * tail
        lead_size = bias_size + up_rows * up_tail

        def extra_rows(flat):
            lead = flat.shape[:-1]
            pad = -flat.shape[-1] % (16 * piece_width)
            flat = jnp.pad(flat, [(0, 0)] * len(lead) + [(0, pad)])
            return flat.reshape(*lead, -1, piece_width)

        def halves(array):
            view = array.reshape(seq_own, 2, half, width)
            first = lax.dynamic_index_in_dim(view, side, 1, keepdims=False)
            other = lax.dynamic_index_in_dim(view, 1 - side, 1, keepdims=False)
            return first, other

        def send_tokens(first):
            if parts != 4:
                return [first] + [shift(first, step) for step in range(1, parts)]
            two = hop(first, far_pairs)
            low = hop(first, up_pairs)
            high = hop(first, down_pairs)
            ends = hop(two, [(2, 3), (1, 0)])
            rank = lax.axis_index("k")
            low = jnp.where(rank == 0, ends, low)
            high = jnp.where(rank == 3, ends, high)
            return [first, low, two, high]

        def join_tokens(near, other):
            far = [other]
            for step in range(1, parts):
                far.append(swap(near[step]))
            blocks = [jnp.stack([a, b], axis=1) for a, b in zip(near, far)]
            return jnp.stack(blocks).reshape(tokens, width)

        def scatter_tokens(array):
            view = array.reshape(parts, seq_own, 2, half, width)
            met = {}
            for step in [*(step for step in (3, 1, 2) if step < parts), *range(4, parts), 0]:
                near = swap(view[step, :, 1])
                met[step] = view[step, :, 0].astype(F32) + near.astype(F32)
            total = met[0]
            if parts != 4:
                for step in range(1, parts):
                    total = total + shift(met[step].astype(BF), parts - step).astype(F32)
            else:
                ahead, behind = met[3].astype(BF), met[1].astype(BF)
                last = hop(ahead, [(3, 2)])
                first = hop(behind, [(0, 1)])
                low = hop(ahead, up_pairs)
                high = hop(behind, down_pairs)
                middle = met[2] + last.astype(F32) + first.astype(F32)
                two = hop(middle.astype(BF), far_pairs)
                total = total + low.astype(F32) + high.astype(F32) + two.astype(F32)
            total = total.astype(BF)
            far = swap(total)
            low = jnp.where(side == 0, total, far)
            high = jnp.where(side == 0, far, total)
            return jnp.stack([low, high], axis=1).reshape(row_count, width).astype(F32)

        def spread(held):
            return lax.all_gather(held, "t", axis=1, tiled=True)

        def scatter_grad(view):
            return lax.psum_scatter(view, "t", scatter_dimension=1, tiled=True)

        qkv_pieces = qkv_weight.reshape(3, slab, parts, attn_units).transpose(2, 1, 0, 3)
        out_pieces = out_weight.reshape(parts, attn_units, slab).transpose(0, 2, 1)
        same = jnp.concatenate(
            [item.reshape(-1) for item in (norm_gain, norm_bias, attn_bias, mlp_bias)]
        )
        small = jnp.concatenate(
            [
                qkv_bias.reshape(3, parts, head_own * tail).transpose(1, 0, 2).reshape(parts, -1),
                up_bias.reshape(parts, -1),
                jnp.broadcast_to(same, (parts, same.size)),
            ],
            axis=-1,
        )
        attn_pieces = jnp.concatenate(
            [
                jnp.concatenate(
                    [qkv_pieces.reshape(parts, slab, 3 * attn_units), out_pieces], axis=-1
                ),
                extra_rows(small),
            ],
            axis=1,
        )
        attn_sent = send_pieces(attn_pieces)
        first_in, other_in = halves(layer_in)
        in_sent = send_tokens(first_in)
        up_sent = send_pieces(up_weight.reshape(slab, parts, hidden).transpose(1, 0, 2))
        down_sent = send_pieces(down_weight.reshape(parts, hidden, slab).transpose(0, 2, 1))
        first_grad, other_grad = halves(out_grad)
        grad_sent = send_tokens(first_grad)

        attn_full = spread(place(attn_sent)).reshape(parts, lanes, -1, piece_width)
        tokens_in = join_tokens(in_sent, other_in)
        up_all = spread(place(up_sent)).reshape(width, hidden)
        down_all = spread(place(down_sent)).reshape(width, hidden)
        tokens_grad = join_tokens(grad_sent, other_grad)

        attn_all = attn_full[:, :, :slab].reshape(width, piece_width)
        qkv_all = attn_all[:, : 3 * attn_units]
        out_all = attn_all[:, 3 * attn_units :]
        small_all = attn_full[:, :, slab:].reshape(devices, -1)
        qkv_shift = (
            small_all[:, :bias_size]
            .reshape(devices, 3 * head_own, tail)
            .transpose(1, 0, 2)
            .reshape(3 * attn_units)
        )
        up_shift = (
            small_all[:, bias_size:lead_size]
            .reshape(devices, up_rows, up_tail)
            .transpose(1, 0, 2)
            .reshape(hidden)
        )
        same_all = (
            small_all[:, lead_size : lead_size + same.size]
            .reshape(devices, 6, slab)
            .transpose(1, 0, 2)
            .reshape(6, width)
            .astype(F32)
        )
        gains, shifts = same_all[0:2], same_all[2:4]
        attn_shift, mlp_shift = same_all[4], same_all[5]

        unit_rows, _ = normalize(tokens_in.astype(F32))
        normed_attn = (unit_rows * gains[0] + shifts[0]).astype(BF)
        normed_mlp = (unit_rows * gains[1] + shifts[1]).astype(BF)
        position = (jnp.arange(SEQ, dtype=jnp.int32) + side * half) % SEQ
        cosine, sine = rotary(position, ROT // 2, ROT)
        projected = matmul(normed_attn, qkv_all, 1, 0) + qkv_shift.astype(F32)
        shaped = [
            projected[:, i * attn_units : (i + 1) * attn_units].reshape(-1, SEQ, head_own, HEAD)
            for i in range(3)
        ]
        queries = turn(shaped[0], cosine, sine, 1.0).astype(BF)
        keys_rot = turn(shaped[1], cosine, sine, 1.0).astype(BF)
        values = shaped[2].astype(BF)
        context, log_total = attend(queries, keys_rot, values, position)
        context_rows = context.reshape(tokens, attn_units)
        pre_act = matmul(normed_mlp, up_all, 1, 0) + up_shift.astype(F32)
        activated = jax.nn.gelu(pre_act, approximate=False).astype(BF)
        branch_sum = matmul(context_rows, out_all, 1, 1) + matmul(activated, down_all, 1, 1)
        branch_half = branch_sum.astype(BF)
        mixed = scatter_tokens(branch_half)
        layer_out = layer_in.astype(F32) + mixed + attn_shift + mlp_shift

        down_grad = matmul(tokens_grad, activated, 0, 0).astype(BF)
        down_held = scatter_grad(down_grad.reshape(parts, lanes * slab, hidden))
        down_out = place(send_pieces(down_held))
        grad_act = matmul(tokens_grad, down_all, 1, 0)
        grad_pre = grad_act * gelu_slope(pre_act)
        up_bias_grad = jnp.sum(grad_pre, axis=0)
        pre_half = grad_pre.astype(BF)
        up_grad = matmul(normed_mlp, pre_half, 0, 0).astype(BF)
        up_held = scatter_grad(up_grad.reshape(parts, lanes * slab, hidden))
        up_out = place(send_pieces(up_held))
        grad_normed_mlp = matmul(pre_half, up_all, 1, 1)

        grad_context = matmul(tokens_grad, out_all, 1, 0).astype(BF).reshape(context.shape)
        grad_queries, grad_keys, grad_values = attend_back(
            queries, keys_rot, values, log_total, grad_context, position
        )
        grad_proj = jnp.concatenate(
            [
                turn(grad_queries, cosine, sine, -1.0).reshape(tokens, attn_units),
                turn(grad_keys, cosine, sine, -1.0).reshape(tokens, attn_units),
                grad_values.reshape(tokens, attn_units),
            ],
            axis=-1,
        )
        qkv_bias_grad = jnp.sum(grad_proj, axis=0)
        proj_half = grad_proj.astype(BF)
        grad_normed_attn = matmul(proj_half, qkv_all, 1, 1)
        out_bias_grad = jnp.sum(
            tokens_grad.reshape(parts, seq_own, 2, half, width)[0, :, 0].astype(F32), axis=(0, 1)
        )
        vectors = jnp.stack(
            [
                jnp.sum(grad_normed_attn * unit_rows, axis=0),
                jnp.sum(grad_normed_mlp * unit_rows, axis=0),
                jnp.sum(grad_normed_attn, axis=0),
                jnp.sum(grad_normed_mlp, axis=0),
                out_bias_grad,
            ]
        )
        grad_unit = scatter_tokens(
            (grad_normed_attn * gains[0] + grad_normed_mlp * gains[1]).astype(BF)
        )
        small_grad = jnp.concatenate(
            [
                qkv_bias_grad.reshape(3 * head_own, devices, tail)
                .transpose(1, 0, 2)
                .reshape(devices, -1),
                up_bias_grad.reshape(up_rows, devices, up_tail)
                .transpose(1, 0, 2)
                .reshape(devices, -1),
                vectors.reshape(5, devices, slab).transpose(1, 0, 2).reshape(devices, -1),
            ],
            axis=-1,
        )
        attn_grad = jnp.concatenate(
            [
                matmul(normed_attn, proj_half, 0, 0).astype(BF),
                matmul(tokens_grad, context_rows, 0, 0).astype(BF),
            ],
            axis=-1,
        )
        attn_held = scatter_grad(attn_grad.reshape(parts, lanes * slab, piece_width))
        attn_out = place(send_pieces(attn_held))

        own_unit, inv_std = normalize(layer_in.astype(F32))
        in_grad = out_grad.astype(F32) + inv_std * (
            grad_unit
            - jnp.mean(grad_unit, axis=-1, keepdims=True)
            - own_unit * jnp.mean(grad_unit * own_unit, axis=-1, keepdims=True)
        )

        small_out = lax.all_to_all(small_grad, ("k", "t"), 0, 0, tiled=True)
        small_out = jnp.sum(small_out.reshape(parts, lanes, -1), axis=1)
        shared = jnp.sum(small_out[:, lead_size : lead_size + 5 * slab], axis=0)
        other = swap(shared)
        shared = (shared + other).reshape(5, slab)
        qkv_bias_out = (
            small_out[:, :bias_size]
            .reshape(parts, 3, head_own, tail)
            .transpose(1, 0, 2, 3)
            .reshape(3, heads, tail)
        )
        up_bias_out = small_out[:, bias_size:lead_size].reshape(parts * up_rows, up_tail)
        qkv_out = (
            attn_out[:, :, : 3 * attn_units]
            .reshape(parts, slab, 3, attn_units)
            .transpose(2, 1, 0, 3)
            .reshape(3, slab, parts * attn_units)
            .astype(F32)
        )
        out_weight_out = (
            attn_out[:, :, 3 * attn_units :]
            .transpose(0, 2, 1)
            .reshape(parts * attn_units, slab)
            .astype(F32)
        )
        up_weight_out = up_out.transpose(1, 0, 2).reshape(slab, parts * hidden).astype(F32)
        down_weight_out = down_out.transpose(0, 2, 1).reshape(parts * hidden, slab).astype(F32)
        return (
            layer_out,
            in_grad,
            shared[0:2],
            shared[2:4],
            qkv_out,
            qkv_bias_out,
            out_weight_out,
            shared[4],
            up_weight_out,
            up_bias_out,
            down_weight_out,
        )

    return body


def solution(mesh):
    data = mesh.shape["dp"]
    model = mesh.shape["mp"]
    dp = ("k", "t")

    def run(*arrays):
        heads = arrays[5].shape[1] // model
        parts = math.gcd(heads, data)
        lanes = data // parts
        fine = Mesh(mesh.devices.reshape(parts, lanes, model), ("k", "t", "mp"))
        placed = (
            P(dp, None),
            P(dp, None),
            P(None, dp),
            P(None, dp),
            P(None, dp, "mp"),
            P(None, "mp", dp),
            P("mp", dp),
            P(dp),
            P(dp, "mp"),
            P("mp", dp),
            P("mp", dp),
            P(dp),
        )
        inner = make_body(parts, lanes)

        return jax.shard_map(
            inner,
            mesh=fine,
            in_specs=placed,
            out_specs=(
                P(dp, None),
                P(dp, None),
                P(None, dp),
                P(None, dp),
                P(None, dp, "mp"),
                P(None, "mp", dp),
                P("mp", dp),
                P(dp),
                P(dp, "mp"),
                P("mp", dp),
                P("mp", dp),
            ),
            check_vma=False,
        )(*arrays)

    return run
```
